32 devices in a mesh: row: 8 (over z, core), rep: 4 (over y, x).
Axes of the slice: x: 2, y: 2, z: 4, core: 2. Of those that a mesh axis runs over, the one named last changes fastest.
Arguments:
- features: bfloat16 [4096, 256], P(('row', 'rep')), may hold values from -6 to 6
- weight: bfloat16 [256, 256], replicated, may hold values from -0.375 to 0.375
- cotangent: bfloat16 [4096, 256], P(('row', 'rep')), may hold values from -6 to 6
- adjacency: bfloat16 [8, 4, 24, 128, 128], P('row', 'rep'), may hold values from -0.15625 to 0.15625
- tile_out: int32 [8, 4, 24], P('row', 'rep'), may hold values from 0 to 3
- tile_in: int32 [8, 4, 24], P('row', 'rep'), may hold values from 0 to 7
- live_count: int32 [8, 4], P('row', 'rep'), may hold values from 6 to 24, as said below
Outputs:
- activated: bfloat16 [4096, 256], P(('row', 'rep'))
- weight_grad: float32 [256, 256], replicated
- feature_grad: float32 [4096, 256], P(('row', 'rep'))
The draws below stay inside these ranges and needn't reach their ends.
Inputs may be any that keep to these rules, and one draw needn't show every extreme that they name: `live_count`: live tile slots of one device; some device has all 24 slots live in every draw.
All inputs are finite; a program needn't handle non-finite values.
Results may differ from the reference program's by a relative error of at most 0.02.
Values may be sent and summed in bfloat16 or wider, within the bound.
A program may use at most 64 MiB of HBM per device.

```python
import jax
import jax.numpy as jnp
from jax import lax

FEAT = 256
BLOCK = 128
SLOTS = 24
NODES = 4096
N_ROW = 8
N_REP = 4


def draw_live_count(key, part):
    first_key = jax.random.fold_in(key, 11)
    second_key = jax.random.fold_in(key, 23)
    counts = jax.random.randint(first_key, (N_ROW * N_REP,), SLOTS // 4, SLOTS + 1)
    chosen = jax.random.randint(second_key, (), 0, N_ROW * N_REP)
    counts = jnp.where(jnp.arange(N_ROW * N_REP) == chosen, SLOTS, counts)
    return counts.reshape(N_ROW, N_REP).astype(jnp.int32)


def with_ends(array, own_key, smallest, high):
    longest = array.shape.index(max(array.shape))
    spots = []
    for shift in (0, 1):
        where = [jax.random.randint(jax.random.fold_in(own_key, axis), (), 0, length) for axis, length in enumerate(array.shape)]
        where[longest] = (where[longest] + shift) % array.shape[longest]
        spots.append(tuple(where))
    return array.at[spots[0]].set(smallest).at[spots[1]].set(high)


def steps_of(own_key, shape, split, least, high):
    loudness = 1.0
    for dim, blocks in split:
        draws = jax.random.uniform(jax.random.fold_in(jax.random.fold_in(own_key, 6), dim), (blocks,), jnp.float32, least / len(split), high / len(split))
        loudness = loudness * jnp.repeat(jnp.exp(draws), shape[dim] // blocks).reshape((-1,) + (1,) * (len(shape) - 1 - dim))
    return loudness


def centred(rng, shape, scale, bound, pieces=(), dtype=jnp.bfloat16):
    entries = scale * jax.random.normal(rng, shape, jnp.float32)
    if pieces:
        entries = entries * steps_of(rng, shape, pieces, -0.22, 0.18)
    return jnp.clip(entries, -bound, bound).astype(dtype)


def setup_inputs(seed: int = 0) -> dict:
    key_of = jax.random.split(jax.random.key(seed), 8)
    features = centred(key_of[0], (NODES, FEAT), 1.0, 6.0, ((0, 32),))
    weight = centred(key_of[1], (FEAT, FEAT), FEAT ** -0.5, 0.375)
    cotangent = centred(key_of[2], (NODES, FEAT), 1.0, 6.0, ((0, 32),))
    adjacency = centred(key_of[3], (N_ROW, N_REP, SLOTS, BLOCK, BLOCK), (SLOTS * BLOCK // 2) ** -0.5, 0.15625, ((0, 8), (1, 4)))
    tile_out = with_ends(jax.random.randint(key_of[4], (N_ROW, N_REP, SLOTS), 0, N_REP), jax.random.fold_in(key_of[4], 1), 0, N_REP - 1).astype(jnp.int32)
    tile_in = with_ends(jax.random.randint(key_of[5], (N_ROW, N_REP, SLOTS), 0, N_ROW), jax.random.fold_in(key_of[5], 1), 0, N_ROW - 1).astype(jnp.int32)
    live_count = draw_live_count(jax.random.fold_in(key_of[7], 71), 0)
    return dict(features=features, weight=weight, cotangent=cotangent, adjacency=adjacency, tile_out=tile_out, tile_in=tile_in, live_count=live_count)


def reference(features, weight, cotangent, adjacency, tile_out, tile_in, live_count):
    blocks = features.reshape(N_ROW, N_REP, BLOCK, FEAT)
    slot_ids = jnp.arange(SLOTS)

    def device_forward(row_id, rep_id):
        tile_set = adjacency[row_id, rep_id].astype(jnp.float32)
        in_ids = tile_in[row_id, rep_id]
        out_ids = tile_out[row_id, rep_id]
        live_mask = (slot_ids < live_count[row_id, rep_id]).astype(jnp.float32)
        column = lax.dynamic_index_in_dim(blocks, rep_id, 1, keepdims=False)
        inputs = column[in_ids].astype(jnp.float32)
        products = jnp.einsum("tij,tjf->tif", tile_set, inputs)
        onehot = (out_ids[None, :] == jnp.arange(N_REP)[:, None]).astype(jnp.float32) * live_mask[None, :]
        summed = jnp.einsum("bt,tif->bif", onehot, products, precision=lax.Precision.HIGHEST)
        return summed.astype(jnp.bfloat16)

    def row_forward(row_id):
        parts = lax.map(lambda rep_id: device_forward(row_id, rep_id), jnp.arange(N_REP))
        return jnp.sum(parts.astype(jnp.float32), axis=0)

    summed_all = lax.map(row_forward, jnp.arange(N_ROW))
    aggregated = summed_all.reshape(NODES, FEAT).astype(jnp.bfloat16)
    pre = jnp.dot(aggregated, weight, preferred_element_type=jnp.float32)
    sig = jax.nn.sigmoid(pre)
    activated = (pre * sig).astype(jnp.bfloat16)
    grad_pre = (cotangent.astype(jnp.float32) * sig * (1.0 + pre * (1.0 - sig))).astype(jnp.bfloat16)
    weight_grad = jnp.dot(aggregated.T, grad_pre, preferred_element_type=jnp.float32)
    grad_rows = jnp.dot(grad_pre, weight.T, preferred_element_type=jnp.float32).astype(jnp.bfloat16)
    grad_blocks = grad_rows.reshape(N_ROW, N_REP, BLOCK, FEAT)

    def device_back(row_id, rep_id):
        tile_set = adjacency[row_id, rep_id].astype(jnp.float32)
        in_ids = tile_in[row_id, rep_id]
        out_ids = tile_out[row_id, rep_id]
        live_mask = (slot_ids < live_count[row_id, rep_id]).astype(jnp.float32)
        group_rows = lax.dynamic_index_in_dim(grad_blocks, row_id, 0, keepdims=False)
        rows_in = group_rows[out_ids].astype(jnp.float32)
        products = jnp.einsum("tji,tjf->tif", tile_set, rows_in)
        onehot = (in_ids[None, :] == jnp.arange(N_ROW)[:, None]).astype(jnp.float32) * live_mask[None, :]
        summed = jnp.einsum("qt,tif->qif", onehot, products, precision=lax.Precision.HIGHEST)
        return summed.astype(jnp.bfloat16)

    def column_back(rep_id):
        def add_row(running, row_id):
            return running + device_back(row_id, rep_id).astype(jnp.float32), None
        start = jnp.zeros((N_ROW, BLOCK, FEAT), jnp.float32)
        running, unused = lax.scan(add_row, start, jnp.arange(N_ROW))
        return running

    returned = lax.map(column_back, jnp.arange(N_REP))
    feature_grad = jnp.transpose(returned, (1, 0, 2, 3)).reshape(NODES, FEAT)
    return activated, weight_grad, feature_grad
```

```python
import functools
import math

import jax
import jax.numpy as jnp
from jax import lax
from jax.experimental import pallas as pl
from jax.experimental.pallas import tpu as pltpu
from jax.sharding import PartitionSpec as P

MESH = pl.DeviceIdType.MESH
F32 = jnp.float32
BF16 = jnp.bfloat16


def each(first, last, step):
    if last - first <= 4:
        for index in range(first, last):
            step(index)
    else:
        lax.fori_loop(first, last, lambda index, unused: (step(index), unused)[1], 0)


def dot(left, right):
    return jnp.dot(left, right, preferred_element_type=F32)


def grid_of(count):
    across = max(n for n in range(1, math.isqrt(count) + 1) if count % n == 0)
    return across, count // across


def kernel(
    Z, C, S,
    feat_hbm, weight_hbm, cot_hbm, adj_hbm, tout_hbm, tin_hbm, live_ref,
    act_ref, wgrad_ref, fgrad_ref,
    tiles, cum, fwd_adj, bwd_adj, feat, weight_ref, cot_ref,
    acc, own_part, part_send, part_recv, grads,
    pair_send, pair_recv, ret_send, ret_recv,
    w_part, w_pair_send, w_pair_recv, w_half, w_rep_send, w_rep_recv, w_z, w_all,
    tout_ref, tin_ref, pos,
    ready, token, local_sem, feat_send_sem, feat_fwd_sem, feat_recv_sem,
    part_send_sem, part_recv_sem, grad_send_sem, grad_recv_sem,
    pair_send_sem, pair_recv_sem, ret_send_sem, ret_recv_sem,
    w_pair_sem, w_rep_sem, w_z_sem, w_gather_sem,
):
    r = lax.axis_index("row")
    c = lax.axis_index("rep")
    z = r // 2
    k = r % 2
    pr = 2 * z + 1 - k
    B = tiles.shape[1]
    W = feat.shape[3]
    halves = feat.shape[0]
    CY, CX = grid_of(C)

    def cols(h):
        return slice(h * W, (h + 1) * W)

    def c_at(e):
        return (c // CX + e // CX) % CY * CX + (c % CX + e % CX) % CX

    def c_from(e):
        return (c // CX + CY - e // CX) % CY * CX + (c % CX + CX - e % CX) % CX

    def far_first(step):
        each(1, C, lambda i: step(C - i))

    def other(j):
        high = 2 * z // Z
        down = Z - j - (z + j) // Z
        up = j - 1 + (j - 1 - z + Z) // Z
        return (1 - high) * down + high * up

    far_end = (1 - 2 * z // Z) * (Z - 1)

    def remote(src, dst, send_sem, recv_sem, **where):
        return pltpu.make_async_remote_copy(
            src_ref=src, dst_ref=dst, send_sem=send_sem, recv_sem=recv_sem,
            device_id=where, device_id_type=MESH,
        )

    def to_partner(src, dst, send_sem, recv_sem):
        return remote(src, dst, send_sem, recv_sem, row=pr)

    barrier = pltpu.get_barrier_semaphore()
    near = sorted({1 % CX, CX - 1, 1 % CY * CX, (CY - 1) * CX} - {0})
    rounds = CY // 2 + CX // 2 - 1

    def greet(semaphore, **where):
        pl.semaphore_signal(semaphore, inc=1, device_id=where, device_id_type=MESH)

    def on_sides(step):
        @pl.when(z < Z - 1)
        def _():
            step(1)

        @pl.when(z > 0)
        def _():
            step(0)

    def side_row(side):
        return 2 * (z + 2 * side - 1) + k

    on_sides(lambda side: greet(barrier, row=side_row(side)))
    greet(barrier, row=pr)
    for e in near:
        greet(barrier, rep=c_at(e))

    own_copies = [
        pltpu.make_async_copy(feat_hbm.at[:, cols(h)], feat.at[h, r], local_sem.at[5])
        for h in range(halves)
    ]
    tile_copy = pltpu.make_async_copy(adj_hbm.at[0, 0], tiles, local_sem.at[0])
    weight_copy = pltpu.make_async_copy(weight_hbm, weight_ref, local_sem.at[1])
    cot_copy = pltpu.make_async_copy(cot_hbm, cot_ref, local_sem.at[2])
    id_copies = [
        pltpu.make_async_copy(tout_hbm, tout_ref, local_sem.at[3]),
        pltpu.make_async_copy(tin_hbm, tin_ref, local_sem.at[4]),
    ]
    for copy in id_copies + [tile_copy] + own_copies + [weight_copy, cot_copy]:
        copy.start()
    sides = (z + Z - 1) // Z + (2 * Z - 2 - z) // Z
    pl.semaphore_wait(barrier, 1 + sides + len(near))

    def feat_copy(h, zz):
        return remote(
            feat_hbm.at[:, cols(h)], feat.at[h, r], feat_send_sem.at[0], feat_recv_sem.at[h, r],
            row=2 * zz + k,
        )

    def feat_forward(h, zz):
        there = feat.at[h, 2 * zz + k]
        return to_partner(there, there, feat_fwd_sem.at[0], feat_recv_sem.at[h, 2 * zz + k])

    def feat_wait(h, q):
        there = feat.at[h, q]
        to_partner(there, there, feat_fwd_sem.at[0], feat_recv_sem.at[h, q]).wait_recv()

    def send_feats(h, d):
        @pl.when(z + d < Z)
        def _():
            feat_copy(h, z + d).start()

        @pl.when(z >= d)
        def _():
            feat_copy(h, z - d).start()

    def pass_token(d):
        on_sides(lambda side: greet(token.at[d], row=side_row(side)))

    def await_token(d):
        pl.semaphore_wait(token.at[d], sides)

    for h in range(halves):
        send_feats(h, 1)
        to_partner(
            feat_hbm.at[:, cols(h)], feat.at[h, r], feat_fwd_sem.at[0], feat_recv_sem.at[h, r]
        ).start()
    if Z > 2:
        pass_token(0)
    if rounds:
        for e in near:
            greet(ready.at[0], rep=c_at(e))

    for copy in id_copies:
        copy.wait()
    live = live_ref[0, 0]
    for s in range(S):
        pos[s] = jnp.where(s < live, tin_ref[0, 0, s] * C + tout_ref[0, 0, s], -1)
    tile_copy.wait()
    cum[S] = jnp.zeros((B, B), F32)
    for s in range(S):
        prev = jnp.int32(S)
        for other_s in range(s):
            prev = jnp.where(pos[other_s] == pos[s], other_s, prev)
        term = tiles[s].astype(F32)
        cum[s] = term + cum[prev] if s else term

    def send_farther(d):
        await_token(d - 2)

        @pl.when(d < Z - 1)
        def _():
            pass_token(d - 1)

        send_feats(0, d)

    each(2, Z, send_farther)
    for h in range(1, halves):
        each(2, Z, lambda d: send_feats(h, d))

    def place(zz, unused):
        for kk in range(2):
            for b in range(C):
                spot = (2 * zz + kk) * C + b
                last = jnp.int32(S)
                for s in range(S):
                    last = jnp.where(pos[s] == spot, s, last)
                block = cum[last]
                fwd_adj[zz, b * B:(b + 1) * B, kk * B:(kk + 1) * B] = block.astype(BF16)
                bwd_adj[2 * zz + kk, :, b * B:(b + 1) * B] = block.T.astype(BF16)
        return unused

    lax.fori_loop(0, Z, place, 0)

    def relay(h, j):
        zz = other(j)
        feat_wait(h, 2 * zz + k)
        feat_forward(h, zz).start()

    def pair_feats(h, zz):
        return feat[h, pl.ds(2 * zz, 2)].reshape(2 * B, W)

    def chip_term(zz):
        for h in range(halves):
            feat_wait(h, 2 * zz + 1 - k)
        both = jnp.concatenate([pair_feats(h, zz) for h in range(halves)], axis=1)
        return dot(fwd_adj[zz], both)

    def add_chip(j):
        acc[...] += chip_term(other(j))

    def relay_all(j):
        for h in range(halves):
            relay(h, j)

    each(3, Z, lambda i: relay_all(Z + 2 - i))
    pltpu.make_async_copy(feat.at[:, r], feat.at[:, r], local_sem.at[5]).wait()
    acc[...] = chip_term(z)
    for j in range(min(2, Z - 1), 0, -1):
        relay(0, j)
    each(3, Z, lambda i: add_chip(Z + 2 - i))
    for j in range(rounds):
        if j:
            for e in near:
                greet(ready.at[j], rep=c_at(e))
        pl.semaphore_wait(ready.at[j], len(near))

    def part_copy(h, e):
        return remote(
            part_send.at[h, e], part_recv.at[h, e], part_send_sem.at[0],
            part_recv_sem.at[h], rep=c_at(e),
        )

    for h in range(halves):
        if Z > 2:
            if h + 1 < halves:
                relay(h + 1, 2)
            feat_wait(h, 2 * other(2) + 1 - k)
            acc[:, cols(h)] += dot(fwd_adj[other(2)], pair_feats(h, other(2)))
        feat_wait(h, 2 * far_end + 1 - k)

        def part_of(b):
            rows = pl.ds(pl.multiple_of(b * B, B), B)
            return acc[rows, cols(h)] + dot(fwd_adj[far_end, rows], pair_feats(h, far_end))

        def send_part(e):
            part_send[h, e] = part_of(c_at(e)).astype(BF16)
            part_copy(h, e).start()

        far_first(send_part)
        if h + 1 < halves:
            relay(h + 1, 1)
        own_part[h] = part_of(c)

    weight_copy.wait()
    cot_copy.wait()
    weight = weight_ref[...]
    pre = None
    agg_halves = []
    for h in range(halves):

        came = part_recv.at[h, pl.ds(1, C - 1)]
        remote(came, came, part_send_sem.at[0], part_recv_sem.at[h], rep=c_at(1)).wait_recv()
        total = own_part[h]
        for e in range(1, C):
            total += part_recv[h, e].astype(F32)
        agg_half = total.astype(BF16)
        agg_halves.append(agg_half)
        term = dot(agg_half, weight[cols(h)])
        pre = term if pre is None else pre + term

    sig = jax.nn.sigmoid(pre)
    grad_pre = (cot_ref[...].astype(F32) * sig * (1.0 + pre * (1.0 - sig))).astype(BF16)

    def grad_copy(h, e):
        return remote(
            grads.at[h, c], grads.at[h, c], grad_send_sem.at[0], grad_recv_sem.at[h],
            rep=c_at(e),
        )

    def make_grads(h):
        grads[h, c] = lax.dot_general(
            grad_pre, weight[cols(h)], (((1,), (1,)), ((), ())), preferred_element_type=F32
        ).astype(BF16)

    def grad_wait(h):
        came = grads.at[h, pl.ds(0, C - 1)]
        remote(came, came, grad_send_sem.at[0], grad_recv_sem.at[h], rep=c_at(1)).wait_recv()

    def send_grads(h):
        far_first(lambda e: grad_copy(h, e).start())

    make_grads(0)
    send_grads(0)

    agg = jnp.concatenate(agg_halves, axis=1)
    w_part[...] = lax.dot_general(
        agg, grad_pre, (((0,), (0,)), ((), ())), preferred_element_type=F32
    ).reshape(w_part.shape)
    w_pair_send[...] = w_part[1 - k].astype(BF16)
    w_pair = to_partner(w_pair_send, w_pair_recv, w_pair_sem.at[0], w_pair_sem.at[1])
    w_pair.start()
    for h in range(1, halves):
        make_grads(h)
    act_ref[...] = (pre * sig).astype(BF16)

    w_pair.wait_recv()
    w_half[...] = w_part[k] + w_pair_recv[...].astype(F32)
    w_rep_send[...] = w_half[...].astype(BF16)

    def w_rep_copy(e):
        return remote(
            w_rep_send.at[c_at(e)], w_rep_recv.at[e], w_rep_sem.at[0], w_rep_sem.at[1],
            rep=c_at(e),
        )

    far_first(lambda e: w_rep_copy(e).start())
    for h in range(1, halves):
        send_grads(h)

    def ends(sent, semaphore):
        remote(sent, sent, semaphore, semaphore, row=pr).wait_send()

    ends(feat.at[:, pl.ds(0, Z - 1)], feat_send_sem.at[0])
    ends(feat.at[:, pl.ds(0, Z)], feat_fwd_sem.at[0])
    ends(part_send.at[:, pl.ds(1, C - 1)], part_send_sem.at[0])

    def returned(h, q):
        return dot(bwd_adj[q], grads[h].reshape(C * B, W))

    def pair_copy(h, zz):
        return to_partner(
            pair_send.at[h, zz], pair_recv.at[h, zz], pair_send_sem.at[0],
            pair_recv_sem.at[h, zz],
        )

    def ret_copy(h, zz):
        return remote(
            ret_send.at[h, zz], ret_recv.at[h, z], ret_send_sem.at[0], ret_recv_sem.at[h],
            row=2 * zz + k,
        )

    def w_z_copy(zz):
        return remote(
            w_z.at[z], w_z.at[z], w_z_sem.at[0], w_z_sem.at[1], row=2 * zz + k
        )

    def return_half(h):
        def send_pair(zz):
            pair_send[h, zz] = returned(h, 2 * zz + 1 - k).astype(BF16)
            pair_copy(h, zz).start()

        def joined(zz):
            value = returned(h, 2 * zz + k)
            pair_copy(h, zz).wait_recv()
            return value + pair_recv[h, zz].astype(F32)

        def send_ret(j):
            zz = other(j)
            ret_send[h, zz] = joined(zz).astype(BF16)
            ret_copy(h, zz).start()

        grad_wait(h)
        each(1, Z, lambda j: send_pair(other(j)))
        send_pair(z)
        if h == 0:
            send_w_z()
        each(1, Z, send_ret)
        fgrad_ref[:, cols(h)] = joined(z)

    def send_w_z():
        came = w_rep_recv.at[pl.ds(1, C - 1)]
        remote(came, came, w_rep_sem.at[0], w_rep_sem.at[1], rep=c_at(1)).wait_recv()
        total = w_half[c]
        for e in range(1, C):
            total += w_rep_recv[e].astype(F32)
        w_z[z] = total.astype(BF16)
        each(1, Z, lambda j: w_z_copy(other(j)).start())

    for h in range(halves):
        return_half(h)

    came = w_z.at[pl.ds(0, Z - 1)]
    remote(came, came, w_z_sem.at[0], w_z_sem.at[1], row=pr).wait_recv()
    w_all[k * C + c] = jnp.sum(w_z[...].astype(F32), axis=0).astype(BF16)

    def w_gather_copy(kk, e):
        mine = w_all.at[k * C + c]
        return remote(
            mine, mine, w_gather_sem.at[0], w_gather_sem.at[1],
            row=2 * z + (k + kk) % 2, rep=c_at(e),
        )

    for kk in range(2):
        each(1 - kk, C, lambda e: w_gather_copy(kk, e).start())

    w_pair.wait_send()
    ends(grads.at[:, pl.ds(0, C - 1)], grad_send_sem.at[0])
    ends(pair_send, pair_send_sem.at[0])
    ends(w_rep_send.at[pl.ds(0, C - 1)], w_rep_sem.at[0])
    ends(w_z.at[pl.ds(0, Z - 1)], w_z_sem.at[0])
    ends(ret_send.at[:, pl.ds(0, Z - 1)], ret_send_sem.at[0])
    most = w_all.at[pl.ds(0, 2 * C - 1)]
    ends(most, w_gather_sem.at[0])

    for h in range(halves):
        came = ret_recv.at[h, pl.ds(0, Z - 1)]
        remote(came, came, ret_send_sem.at[0], ret_recv_sem.at[h], row=pr).wait_recv()
        total = fgrad_ref[:, cols(h)]
        for j in range(1, Z):
            total += ret_recv[h, other(j)].astype(F32)
        fgrad_ref[:, cols(h)] = total
    remote(most, most, w_gather_sem.at[0], w_gather_sem.at[1], row=pr).wait_recv()
    wgrad_ref[...] = w_all[...].astype(F32).reshape(wgrad_ref.shape)


def write_out(*refs):
    count = len(refs) // 2
    sem = refs[-1]
    copies = [
        pltpu.make_async_copy(refs[i], refs[count + i], sem.at[i]) for i in range(count)
    ]
    for copy in copies:
        copy.start()
    for copy in copies:
        copy.wait()


def solution(mesh):
    R = mesh.shape["row"]
    C = mesh.shape["rep"]
    Z = R // 2

    def body(features, weight, cotangent, adjacency, tile_out, tile_in, live_count):
        B, F = features.shape
        S = adjacency.shape[2]
        H = F // (2 * C)
        N = 2
        W = F // N
        CY, CX = grid_of(C)
        anywhere = pl.BlockSpec(memory_space=pl.ANY)
        vector = pl.BlockSpec(memory_space=pltpu.VMEM)
        dma = pltpu.SemaphoreType.DMA
        out_shape = (
            jax.ShapeDtypeStruct((B, F), BF16),
            jax.ShapeDtypeStruct(weight.shape, F32),
            jax.ShapeDtypeStruct((B, F), F32),
        )
        buffers = [
            ((S, B, B), BF16), ((S + 1, B, B), F32),
            ((Z, C * B, 2 * B), BF16), ((R, B, C * B), BF16),
            ((N, R, B, W), BF16), (weight.shape, BF16), ((B, F), BF16),
            ((C * B, F), F32), ((N, B, W), F32),
            ((N, C, B, W), BF16), ((N, C, B, W), BF16), ((N, C, B, W), BF16),
            ((N, Z, B, W), BF16), ((N, Z, B, W), BF16),
            ((N, Z, B, W), BF16), ((N, Z, B, W), BF16),
            ((2, C, H, F), F32), ((C, H, F), BF16), ((C, H, F), BF16), ((C, H, F), F32),
            ((C, H, F), BF16), ((C, H, F), BF16), ((Z, H, F), BF16), ((2 * C, H, F), BF16),
        ]
        held = sum(math.prod(shape) * (4 if kind == F32 else 2) for shape, kind in buffers)
        results = pl.pallas_call(
            functools.partial(kernel, Z, C, S),
            out_shape=out_shape,
            in_specs=[pl.BlockSpec(memory_space=pltpu.HBM)] * 6
            + [pl.BlockSpec(memory_space=pltpu.SMEM)],
            out_specs=(vector, vector, vector),
            scratch_shapes=[pltpu.VMEM(shape, kind) for shape, kind in buffers] + [
                pltpu.SMEM(tile_out.shape, jnp.int32),
                pltpu.SMEM(tile_in.shape, jnp.int32),
                pltpu.SMEM((S,), jnp.int32),
                pltpu.SemaphoreType.REGULAR((max(CY // 2 + CX // 2 - 1, 1),)),
                pltpu.SemaphoreType.REGULAR((max(Z - 2, 1),)),
                dma((6,)), dma((1,)), dma((1,)), dma((N, R)),
                dma((1,)), dma((N,)), dma((1,)), dma((N,)),
                dma((1,)), dma((N, Z)), dma((1,)), dma((N,)),
                dma((2,)), dma((2,)), dma((2,)), dma((2,)),
            ],
            compiler_params=pltpu.CompilerParams(
                collective_id=0, has_side_effects=True,
                vmem_limit_bytes=min(held + 8 * 2 ** 20, 60 * 2 ** 20),
            ),
        )(*(
            pltpu.with_memory_space_constraint(arg, pltpu.HBM)
            for arg in (features, weight, cotangent, adjacency, tile_out, tile_in)
        ), live_count)
        return pl.pallas_call(
            write_out,
            out_shape=out_shape,
            in_specs=[vector] * 3,
            out_specs=(anywhere,) * 3,
            scratch_shapes=[dma((3,))],
            compiler_params=pltpu.CompilerParams(vmem_limit_bytes=4 * 2 ** 20),
        )(*results)

    return jax.shard_map(
        body,
        mesh=mesh,
        in_specs=(
            P(("row", "rep"), None),
            P(),
            P(("row", "rep"), None),
            P("row", "rep", None, None, None),
            P("row", "rep", None),
            P("row", "rep", None),
            P("row", "rep"),
        ),
        out_specs=(P(("row", "rep"), None), P(), P(("row", "rep"), None)),
        check_vma=False,
    )
```

```python
import functools
import math

import jax
import jax.numpy as jnp
from jax import lax
from jax.experimental import pallas as pl
from jax.experimental.pallas import tpu as pltpu
from jax.sharding import PartitionSpec as P

MESH = pl.DeviceIdType.MESH
F32 = jnp.float32
BF16 = jnp.bfloat16


def each(first, last, step):
    if last - first <= 4:
        for index in range(first, last):
            step(index)
    else:
        lax.fori_loop(first, last, lambda index, unused: (step(index), unused)[1], 0)


def dot(left, right):
    return jnp.dot(left, right, preferred_element_type=F32)


def grid_of(count):
    across = max(n for n in range(1, math.isqrt(count) + 1) if count % n == 0)
    return across, count // across


def kernel(
    Z, C, S,
    feat_hbm, weight_hbm, cot_hbm, adj_hbm, tout_hbm, tin_hbm, live_ref,
    act_ref, wgrad_ref, fgrad_ref,
    tiles, cum, fwd_adj, bwd_adj, feat, weight_ref, cot_ref,
    acc, own_part, part_send, part_recv, grads,
    pair_send, pair_recv, ret_send, ret_recv,
    w_part, w_pair_send, w_pair_recv, w_half, w_rep_send, w_rep_recv, w_z, w_all,
    tout_ref, tin_ref, pos,
    ready, token, local_sem, feat_send_sem, feat_fwd_sem, feat_recv_sem,
    part_send_sem, part_recv_sem, grad_send_sem, grad_recv_sem,
    pair_send_sem, pair_recv_sem, ret_send_sem, ret_recv_sem,
    w_pair_sem, w_rep_sem, w_z_sem, w_gather_sem,
):
    r = lax.axis_index("row")
    c = lax.axis_index("rep")
    z = r // 2
    k = r % 2
    pr = 2 * z + 1 - k
    B = tiles.shape[1]
    W = feat.shape[3]
    halves = feat.shape[0]
    CY, CX = grid_of(C)

    def cols(h):
        return slice(h * W, (h + 1) * W)

    def c_at(e):
        return (c // CX + e // CX) % CY * CX + (c % CX + e % CX) % CX

    def c_from(e):
        return (c // CX + CY - e // CX) % CY * CX + (c % CX + CX - e % CX) % CX

    def far_first(step):
        each(1, C, lambda i: step(C - i))

    def other(j):
        high = 2 * z // Z
        down = Z - j - (z + j) // Z
        up = j - 1 + (j - 1 - z + Z) // Z
        return (1 - high) * down + high * up

    def low_first(j):
        first = 1 - (z + Z - 1) // Z
        up = j - 1 + (j - 1 - z + Z) // Z
        return first * (Z - j) + (1 - first) * up

    def low_rep(e):
        return e - 1 + (e - 1 - c + C) // C

    far_end = (1 - 2 * z // Z) * (Z - 1)

    def remote(src, dst, send_sem, recv_sem, **where):
        return pltpu.make_async_remote_copy(
            src_ref=src, dst_ref=dst, send_sem=send_sem, recv_sem=recv_sem,
            device_id=where, device_id_type=MESH,
        )

    def to_partner(src, dst, send_sem, recv_sem):
        return remote(src, dst, send_sem, recv_sem, row=pr)

    barrier = pltpu.get_barrier_semaphore()
    near = sorted({1 % CX, CX - 1, 1 % CY * CX, (CY - 1) * CX} - {0})
    rounds = CY // 2 + CX // 2 - 1

    def greet(semaphore, **where):
        pl.semaphore_signal(semaphore, inc=1, device_id=where, device_id_type=MESH)

    def on_sides(step):
        @pl.when(z < Z - 1)
        def _():
            step(1)

        @pl.when(z > 0)
        def _():
            step(0)

    def side_row(side):
        return 2 * (z + 2 * side - 1) + k

    on_sides(lambda side: greet(barrier, row=side_row(side)))
    greet(barrier, row=pr)
    for e in near:
        greet(barrier, rep=c_at(e))

    own_copies = [
        pltpu.make_async_copy(feat_hbm.at[:, cols(h)], feat.at[h, r], local_sem.at[5])
        for h in range(halves)
    ]
    tile_copy = pltpu.make_async_copy(adj_hbm.at[0, 0], tiles, local_sem.at[0])
    weight_copy = pltpu.make_async_copy(weight_hbm, weight_ref, local_sem.at[1])
    cot_copy = pltpu.make_async_copy(cot_hbm, cot_ref, local_sem.at[2])
    id_copies = [
        pltpu.make_async_copy(tout_hbm, tout_ref, local_sem.at[3]),
        pltpu.make_async_copy(tin_hbm, tin_ref, local_sem.at[4]),
    ]
    for copy in id_copies + [tile_copy] + own_copies + [weight_copy, cot_copy]:
        copy.start()
    sides = (z + Z - 1) // Z + (2 * Z - 2 - z) // Z
    pl.semaphore_wait(barrier, 1 + sides + len(near))

    def feat_copy(h, zz):
        return remote(
            feat_hbm.at[:, cols(h)], feat.at[h, r], feat_send_sem.at[0], feat_recv_sem.at[h, r],
            row=2 * zz + k,
        )

    def feat_forward(h, zz):
        there = feat.at[h, 2 * zz + k]
        return to_partner(there, there, feat_fwd_sem.at[0], feat_recv_sem.at[h, 2 * zz + k])

    def feat_wait(h, q):
        there = feat.at[h, q]
        to_partner(there, there, feat_fwd_sem.at[0], feat_recv_sem.at[h, q]).wait_recv()

    passing = Z > 3

    def send_feats(h, d):
        @pl.when(z + d < Z - (passing and d == 2))
        def _():
            feat_copy(h, z + d).start()

        @pl.when(z >= d + (passing and d == 2))
        def _():
            feat_copy(h, z - d).start()

    def pass_on(h, zz):
        there = feat.at[h, 2 * zz + k]
        return remote(
            there, there, feat_send_sem.at[1], feat_recv_sem.at[h, 2 * zz + k],
            row=2 * (2 * z - zz) + k,
        )

    def at_pass(zz, step):
        if passing:
            @pl.when(jnp.logical_or(
                jnp.logical_and(z == 1, zz == 2), jnp.logical_and(z == Z - 2, zz == Z - 3)
            ))
            def _():
                step()

    def pass_token(d):
        on_sides(lambda side: greet(token.at[d], row=side_row(side)))

    def await_token(d):
        pl.semaphore_wait(token.at[d], sides)

    if Z > 2:
        pass_token(0)
    if rounds:
        for e in near:
            greet(ready.at[0], rep=c_at(e))
    for h in range(halves):
        send_feats(h, 1)
        to_partner(
            feat_hbm.at[:, cols(h)], feat.at[h, r], feat_fwd_sem.at[0], feat_recv_sem.at[h, r]
        ).start()

    for copy in id_copies:
        copy.wait()
    live = live_ref[0, 0]
    for s in range(S):
        pos[s] = jnp.where(s < live, tin_ref[0, 0, s] * C + tout_ref[0, 0, s], -1)
    tile_copy.wait()
    cum[S] = jnp.zeros((B, B), F32)
    for s in range(S):
        prev = jnp.int32(S)
        for other_s in range(s):
            prev = jnp.where(pos[other_s] == pos[s], other_s, prev)
        term = tiles[s].astype(F32)
        cum[s] = term + cum[prev] if s else term

    def send_farther(d):
        await_token(d - 2)

        @pl.when(d < Z - 1)
        def _():
            pass_token(d - 1)

        send_feats(0, d)

    if Z > 2:
        send_farther(2)

    def place(zz, unused):
        for kk in range(2):
            for b in range(C):
                spot = (2 * zz + kk) * C + b
                last = jnp.int32(S)
                for s in range(S):
                    last = jnp.where(pos[s] == spot, s, last)
                block = cum[last]
                fwd_adj[zz, b * B:(b + 1) * B, kk * B:(kk + 1) * B] = block.astype(BF16)
                bwd_adj[2 * zz + kk, :, b * B:(b + 1) * B] = block.T.astype(BF16)
        return unused

    lax.fori_loop(0, Z, place, 0)
    each(3, Z, send_farther)
    for h in range(1, halves):
        each(2, Z, lambda d: send_feats(h, d))

    def relay(h, j):
        zz = other(j)
        feat_wait(h, 2 * zz + k)
        at_pass(zz, lambda: pass_on(h, zz).start())
        feat_forward(h, zz).start()

    def pair_feats(h, zz):
        return feat[h, pl.ds(2 * zz, 2)].reshape(2 * B, W)

    def chip_term(zz):
        for h in range(halves):
            feat_wait(h, 2 * zz + 1 - k)
        both = jnp.concatenate([pair_feats(h, zz) for h in range(halves)], axis=1)
        return dot(fwd_adj[zz], both)

    def add_chip(j):
        acc[...] += chip_term(other(j))

    def relay_all(j):
        for h in range(halves):
            relay(h, j)

    pltpu.make_async_copy(feat.at[:, r], feat.at[:, r], local_sem.at[5]).wait()
    acc[...] = chip_term(z)
    each(3, Z, lambda i: relay_all(Z + 2 - i))
    far = range(1, min(2, Z - 1) + 1)

    @pl.when(jnp.logical_and(z > 0, z < Z - 1))
    def _():
        relay_all(far[-1])

    @pl.when(jnp.logical_or(z == 0, z == Z - 1))
    def _():
        for j in far:
            relay(0, j)

    each(3, Z, lambda i: add_chip(Z + 2 - i))

    @pl.when(jnp.logical_and(z > 0, z < Z - 1))
    def _():
        for j in far[:-1]:
            relay_all(j)

    @pl.when(jnp.logical_or(z == 0, z == Z - 1))
    def _():
        for h in range(1, halves):
            for j in far:
                relay(h, j)

    for j in range(rounds):
        if j:
            for e in near:
                greet(ready.at[j], rep=c_at(e))
        pl.semaphore_wait(ready.at[j], len(near))

    def part_of(h, b):
        rows = pl.ds(pl.multiple_of(b * B, B), B)
        return acc[rows, cols(h)] + dot(fwd_adj[far_end, rows], pair_feats(h, far_end))

    def part_copy(h, e):
        return remote(
            part_send.at[h, e], part_recv.at[h, e], part_send_sem.at[0],
            part_recv_sem.at[h], rep=c_at(e),
        )

    for h in range(halves):
        if Z > 2:
            feat_wait(h, 2 * other(2) + 1 - k)
            acc[:, cols(h)] += dot(fwd_adj[other(2)], pair_feats(h, other(2)))
        feat_wait(h, 2 * far_end + 1 - k)

        def send_part(e):
            part_send[h, e] = part_of(h, c_at(e)).astype(BF16)
            part_copy(h, e).start()

        far_first(send_part)

    for h in range(halves):
        own_part[h] = part_of(h, c)

    weight_copy.wait()
    cot_copy.wait()
    weight = weight_ref[...]
    pre = None
    agg_halves = []
    for h in range(halves):

        came = part_recv.at[h, pl.ds(1, C - 1)]
        remote(came, came, part_send_sem.at[0], part_recv_sem.at[h], rep=c_at(1)).wait_recv()
        total = own_part[h]
        for e in range(1, C):
            total += part_recv[h, e].astype(F32)
        agg_half = total.astype(BF16)
        agg_halves.append(agg_half)
        term = dot(agg_half, weight[cols(h)])
        pre = term if pre is None else pre + term

    sig = jax.nn.sigmoid(pre)
    grad_pre = (cot_ref[...].astype(F32) * sig * (1.0 + pre * (1.0 - sig))).astype(BF16)

    def grad_copy(h, e):
        return remote(
            grads.at[h, c], grads.at[h, c], grad_send_sem.at[0], grad_recv_sem.at[h],
            rep=c_at(e),
        )

    def make_grads(h):
        grads[h, c] = lax.dot_general(
            grad_pre, weight[cols(h)], (((1,), (1,)), ((), ())), preferred_element_type=F32
        ).astype(BF16)

    def grad_wait(h):
        came = grads.at[h, pl.ds(0, C - 1)]
        remote(came, came, grad_send_sem.at[0], grad_recv_sem.at[h], rep=c_at(1)).wait_recv()

    def send_grads(h):
        far_first(lambda e: grad_copy(h, e).start())

    make_grads(0)
    send_grads(0)

    agg = jnp.concatenate(agg_halves, axis=1)
    w_part[...] = lax.dot_general(
        agg, grad_pre, (((0,), (0,)), ((), ())), preferred_element_type=F32
    ).reshape(w_part.shape)
    w_pair_send[...] = w_part[1 - k].astype(BF16)
    w_pair = to_partner(w_pair_send, w_pair_recv, w_pair_sem.at[0], w_pair_sem.at[1])
    w_pair.start()
    for h in range(1, halves):
        make_grads(h)
    act_ref[...] = (pre * sig).astype(BF16)

    w_pair.wait_recv()
    w_half[...] = w_part[k] + w_pair_recv[...].astype(F32)
    w_rep_send[...] = w_half[...].astype(BF16)

    def w_rep_copy(e):
        return remote(
            w_rep_send.at[c_at(e)], w_rep_recv.at[e], w_rep_sem.at[0], w_rep_sem.at[1],
            rep=c_at(e),
        )

    far_first(lambda e: w_rep_copy(e).start())
    for h in range(1, halves):
        send_grads(h)

    def ends(sent, semaphore):
        remote(sent, sent, semaphore, semaphore, row=pr).wait_send()

    skipped = [jnp.logical_and(z == 2, passing), jnp.logical_and(z == Z - 3, passing)]
    for count in range(3):
        @pl.when(sum(jnp.where(one, 1, 0) for one in skipped) == count)
        def _():
            ends(feat.at[:, pl.ds(0, Z - 1 - count)], feat_send_sem.at[0])

    for near_end in (1, Z - 2) if passing else ():
        @pl.when(z == near_end)
        def _():
            ends(feat.at[:, pl.ds(0, 1)], feat_send_sem.at[1])

    ends(feat.at[:, pl.ds(0, Z)], feat_fwd_sem.at[0])
    ends(part_send.at[:, pl.ds(1, C - 1)], part_send_sem.at[0])

    def returned(h, q):
        return dot(bwd_adj[q], grads[h].reshape(C * B, W))

    def pair_copy(h, zz):
        return to_partner(
            pair_send.at[h, zz], pair_recv.at[h, zz], pair_send_sem.at[0],
            pair_recv_sem.at[h, zz],
        )

    def ret_copy(h, zz):
        return remote(
            ret_send.at[h, zz], ret_recv.at[h, z], ret_send_sem.at[0], ret_recv_sem.at[h],
            row=2 * zz + k,
        )

    def w_z_copy(zz):
        return remote(
            w_z.at[z], w_z.at[z], w_z_sem.at[0], w_z_sem.at[1], row=2 * zz + k
        )

    def send_pair(h, zz):
        pair_send[h, zz] = returned(h, 2 * zz + 1 - k).astype(BF16)
        pair_copy(h, zz).start()

    def joined(h, zz):
        value = returned(h, 2 * zz + k)
        pair_copy(h, zz).wait_recv()
        return value + pair_recv[h, zz].astype(F32)

    def send_ret(h, j):
        zz = low_first(j)
        ret_send[h, zz] = joined(h, zz).astype(BF16)
        ret_copy(h, zz).start()

    def send_pairs(h):
        grad_wait(h)
        each(1, Z, lambda j: send_pair(h, low_first(j)))
        send_pair(h, z)

    def own_ret(h):
        fgrad_ref[:, cols(h)] = joined(h, z)

    def send_w_z():
        came = w_rep_recv.at[pl.ds(1, C - 1)]
        remote(came, came, w_rep_sem.at[0], w_rep_sem.at[1], rep=c_at(1)).wait_recv()
        total = w_half[c]
        for e in range(1, C):
            total += w_rep_recv[e].astype(F32)
        w_z[z] = total.astype(BF16)
        each(1, Z, lambda j: w_z_copy(low_first(j)).start())

    held = (Z - 1) // 3
    send_pairs(0)
    send_w_z()
    for h in range(halves):
        each(1 if h == 0 else 2, Z - held if h + 1 < halves else Z, lambda j: send_ret(h, j))
        own_ret(h)
        if h + 1 < halves:
            send_pairs(h + 1)
            send_ret(h + 1, 1)
            each(Z - held, Z, lambda j: send_ret(h, j))

    came = w_z.at[pl.ds(0, Z - 1)]
    remote(came, came, w_z_sem.at[0], w_z_sem.at[1], row=pr).wait_recv()
    w_all[k * C + c] = jnp.sum(w_z[...].astype(F32), axis=0).astype(BF16)

    def w_gather_copy(other_k, dst):
        mine = w_all.at[k * C + c]
        return remote(
            mine, mine, w_gather_sem.at[0], w_gather_sem.at[1],
            row=2 * z + (k + other_k) % 2, rep=dst,
        )

    def w_gather(e):
        for other_k in range(2):
            w_gather_copy(other_k, low_rep(e)).start()

    each(1, C, w_gather)
    w_gather_copy(1, c).start()

    w_pair.wait_send()
    ends(grads.at[:, pl.ds(0, C - 1)], grad_send_sem.at[0])
    ends(pair_send, pair_send_sem.at[0])
    ends(w_rep_send.at[pl.ds(0, C - 1)], w_rep_sem.at[0])
    ends(w_z.at[pl.ds(0, Z - 1)], w_z_sem.at[0])
    ends(ret_send.at[:, pl.ds(0, Z - 1)], ret_send_sem.at[0])
    most = w_all.at[pl.ds(0, 2 * C - 1)]
    ends(most, w_gather_sem.at[0])

    for h in range(halves):
        came = ret_recv.at[h, pl.ds(0, Z - 1)]
        remote(came, came, ret_send_sem.at[0], ret_recv_sem.at[h], row=pr).wait_recv()
        total = fgrad_ref[:, cols(h)]
        for j in range(1, Z):
            total += ret_recv[h, other(j)].astype(F32)
        fgrad_ref[:, cols(h)] = total
    remote(most, most, w_gather_sem.at[0], w_gather_sem.at[1], row=pr).wait_recv()
    wgrad_ref[...] = w_all[...].astype(F32).reshape(wgrad_ref.shape)


def write_out(*refs):
    count = len(refs) // 2
    sem = refs[-1]
    copies = [
        pltpu.make_async_copy(refs[i], refs[count + i], sem.at[i]) for i in range(count)
    ]
    for copy in copies:
        copy.start()
    for copy in copies:
        copy.wait()


def solution(mesh):
    R = mesh.shape["row"]
    C = mesh.shape["rep"]
    Z = R // 2

    def body(features, weight, cotangent, adjacency, tile_out, tile_in, live_count):
        B, F = features.shape
        S = adjacency.shape[2]
        H = F // (2 * C)
        N = 2
        W = F // N
        CY, CX = grid_of(C)
        anywhere = pl.BlockSpec(memory_space=pl.ANY)
        vector = pl.BlockSpec(memory_space=pltpu.VMEM)
        dma = pltpu.SemaphoreType.DMA
        out_shape = (
            jax.ShapeDtypeStruct((B, F), BF16),
            jax.ShapeDtypeStruct(weight.shape, F32),
            jax.ShapeDtypeStruct((B, F), F32),
        )
        buffers = [
            ((S, B, B), BF16), ((S + 1, B, B), F32),
            ((Z, C * B, 2 * B), BF16), ((R, B, C * B), BF16),
            ((N, R, B, W), BF16), (weight.shape, BF16), ((B, F), BF16),
            ((C * B, F), F32), ((N, B, W), F32),
            ((N, C, B, W), BF16), ((N, C, B, W), BF16), ((N, C, B, W), BF16),
            ((N, Z, B, W), BF16), ((N, Z, B, W), BF16),
            ((N, Z, B, W), BF16), ((N, Z, B, W), BF16),
            ((2, C, H, F), F32), ((C, H, F), BF16), ((C, H, F), BF16), ((C, H, F), F32),
            ((C, H, F), BF16), ((C, H, F), BF16), ((Z, H, F), BF16), ((2 * C, H, F), BF16),
        ]
        held = sum(math.prod(shape) * (4 if kind == F32 else 2) for shape, kind in buffers)
        results = pl.pallas_call(
            functools.partial(kernel, Z, C, S),
            out_shape=out_shape,
            in_specs=[pl.BlockSpec(memory_space=pltpu.HBM)] * 6
            + [pl.BlockSpec(memory_space=pltpu.SMEM)],
            out_specs=(vector, vector, vector),
            scratch_shapes=[pltpu.VMEM(shape, kind) for shape, kind in buffers] + [
                pltpu.SMEM(tile_out.shape, jnp.int32),
                pltpu.SMEM(tile_in.shape, jnp.int32),
                pltpu.SMEM((S,), jnp.int32),
                pltpu.SemaphoreType.REGULAR((max(CY // 2 + CX // 2 - 1, 1),)),
                pltpu.SemaphoreType.REGULAR((max(Z - 2, 1),)),
                dma((6,)), dma((2,)), dma((1,)), dma((N, R)),
                dma((1,)), dma((N,)), dma((1,)), dma((N,)),
                dma((1,)), dma((N, Z)), dma((1,)), dma((N,)),
                dma((2,)), dma((2,)), dma((2,)), dma((2,)),
            ],
            compiler_params=pltpu.CompilerParams(
                collective_id=0, has_side_effects=True,
                vmem_limit_bytes=min(held + 8 * 2 ** 20, 60 * 2 ** 20),
            ),
        )(*(
            pltpu.with_memory_space_constraint(arg, pltpu.HBM)
            for arg in (features, weight, cotangent, adjacency, tile_out, tile_in)
        ), live_count)
        return pl.pallas_call(
            write_out,
            out_shape=out_shape,
            in_specs=[vector] * 3,
            out_specs=(anywhere,) * 3,
            scratch_shapes=[dma((3,))],
            compiler_params=pltpu.CompilerParams(vmem_limit_bytes=4 * 2 ** 20),
        )(*results)

    return jax.shard_map(
        body,
        mesh=mesh,
        in_specs=(
            P(("row", "rep"), None),
            P(),
            P(("row", "rep"), None),
            P("row", "rep", None, None, None),
            P("row", "rep", None),
            P("row", "rep", None),
            P("row", "rep"),
        ),
        out_specs=(P(("row", "rep"), None), P(), P(("row", "rep"), None)),
        check_vma=False,
    )
```

```python
import functools
import math

import jax
import jax.numpy as jnp
from jax import lax
from jax.experimental import pallas as pl
from jax.experimental.pallas import tpu as pltpu
from jax.sharding import PartitionSpec as P

MESH = pl.DeviceIdType.MESH
F32 = jnp.float32
BF16 = jnp.bfloat16


def each(first, last, step):
    if last - first <= 4:
        for index in range(first, last):
            step(index)
    else:
        lax.fori_loop(first, last, lambda index, unused: (step(index), unused)[1], 0)


def dot(left, right):
    return jnp.dot(left, right, preferred_element_type=F32)


def grid_of(count):
    across = max(n for n in range(1, math.isqrt(count) + 1) if count % n == 0)
    return across, count // across


def kernel(
    Z, C, S,
    feat_hbm, weight_hbm, cot_hbm, adj_hbm, tout_hbm, tin_hbm, live_ref,
    act_ref, wgrad_ref, fgrad_ref,
    tiles, cum, fwd_adj, bwd_adj, feat, weight_ref, cot_ref,
    acc, own_part, part_send, part_recv, grads,
    pair_send, pair_recv, ret_send, ret_recv,
    w_part, w_pair_send, w_pair_recv, w_half, w_rep_send, w_rep_recv, w_z, w_all,
    tout_ref, tin_ref, pos,
    ready, token, local_sem, feat_send_sem, feat_fwd_sem, feat_recv_sem,
    part_send_sem, part_recv_sem, grad_send_sem, grad_recv_sem,
    pair_send_sem, pair_recv_sem, ret_send_sem, ret_recv_sem,
    w_pair_sem, w_rep_sem, w_z_sem, w_gather_sem,
):
    r = lax.axis_index("row")
    c = lax.axis_index("rep")
    z = r // 2
    k = r % 2
    pr = 2 * z + 1 - k
    B = tiles.shape[1]
    W = feat.shape[3]
    halves = feat.shape[0]
    CY, CX = grid_of(C)

    def cols(h):
        return slice(h * W, (h + 1) * W)

    def c_at(e):
        return (c // CX + e // CX) % CY * CX + (c % CX + e % CX) % CX

    def c_from(e):
        return (c // CX + CY - e // CX) % CY * CX + (c % CX + CX - e % CX) % CX

    def far_first(step):
        each(1, C, lambda i: step(C - i))

    def other(j):
        high = 2 * z // Z
        down = Z - j - (z + j) // Z
        up = j - 1 + (j - 1 - z + Z) // Z
        return (1 - high) * down + high * up

    def low_first(j):
        first = 1 - (z + Z - 1) // Z
        up = j - 1 + (j - 1 - z + Z) // Z
        return first * (Z - j) + (1 - first) * up

    def low_rep(e):
        return e - 1 + (e - 1 - c + C) // C

    far_end = (1 - 2 * z // Z) * (Z - 1)

    def remote(src, dst, send_sem, recv_sem, **where):
        return pltpu.make_async_remote_copy(
            src_ref=src, dst_ref=dst, send_sem=send_sem, recv_sem=recv_sem,
            device_id=where, device_id_type=MESH,
        )

    def to_partner(src, dst, send_sem, recv_sem):
        return remote(src, dst, send_sem, recv_sem, row=pr)

    barrier = pltpu.get_barrier_semaphore()
    near = sorted({1 % CX, CX - 1, 1 % CY * CX, (CY - 1) * CX} - {0})
    rounds = CY // 2 + CX // 2 - 1

    def greet(semaphore, **where):
        pl.semaphore_signal(semaphore, inc=1, device_id=where, device_id_type=MESH)

    def on_sides(step):
        @pl.when(z < Z - 1)
        def _():
            step(1)

        @pl.when(z > 0)
        def _():
            step(0)

    def side_row(side):
        return 2 * (z + 2 * side - 1) + k

    on_sides(lambda side: greet(barrier, row=side_row(side)))
    greet(barrier, row=pr)
    for e in near:
        greet(barrier, rep=c_at(e))

    own_copies = [
        pltpu.make_async_copy(feat_hbm.at[:, cols(h)], feat.at[h, r], local_sem.at[5])
        for h in range(halves)
    ]
    tile_copy = pltpu.make_async_copy(adj_hbm.at[0, 0], tiles, local_sem.at[0])
    weight_copy = pltpu.make_async_copy(weight_hbm, weight_ref, local_sem.at[1])
    cot_copy = pltpu.make_async_copy(cot_hbm, cot_ref, local_sem.at[2])
    id_copies = [
        pltpu.make_async_copy(tout_hbm, tout_ref, local_sem.at[3]),
        pltpu.make_async_copy(tin_hbm, tin_ref, local_sem.at[4]),
    ]
    for copy in id_copies + [tile_copy] + own_copies + [weight_copy, cot_copy]:
        copy.start()
    sides = (z + Z - 1) // Z + (2 * Z - 2 - z) // Z
    pl.semaphore_wait(barrier, 1 + sides + len(near))

    def feat_copy(h, zz):
        return remote(
            feat_hbm.at[:, cols(h)], feat.at[h, r], feat_send_sem.at[0], feat_recv_sem.at[h, r],
            row=2 * zz + k,
        )

    def feat_forward(h, zz):
        there = feat.at[h, 2 * zz + k]
        return to_partner(there, there, feat_fwd_sem.at[0], feat_recv_sem.at[h, 2 * zz + k])

    def feat_wait(h, q):
        there = feat.at[h, q]
        to_partner(there, there, feat_fwd_sem.at[0], feat_recv_sem.at[h, q]).wait_recv()

    passing = Z > 3

    def send_feats(h, d):
        @pl.when(z + d < Z - (passing and d == 2))
        def _():
            feat_copy(h, z + d).start()

        @pl.when(z >= d + (passing and d == 2))
        def _():
            feat_copy(h, z - d).start()

    def pass_on(h, zz):
        there = feat.at[h, 2 * zz + k]
        return remote(
            there, there, feat_send_sem.at[1], feat_recv_sem.at[h, 2 * zz + k],
            row=2 * (2 * z - zz) + k,
        )

    def at_pass(zz, step):
        if passing:
            @pl.when(jnp.logical_or(
                jnp.logical_and(z == 1, zz == 2), jnp.logical_and(z == Z - 2, zz == Z - 3)
            ))
            def _():
                step()

    def pass_token(d):
        on_sides(lambda side: greet(token.at[d], row=side_row(side)))

    def await_token(d):
        pl.semaphore_wait(token.at[d], sides)

    if Z > 2:
        pass_token(0)
    if rounds:
        for e in near:
            greet(ready.at[0], rep=c_at(e))
    for h in range(halves):
        send_feats(h, 1)
        to_partner(
            feat_hbm.at[:, cols(h)], feat.at[h, r], feat_fwd_sem.at[0], feat_recv_sem.at[h, r]
        ).start()

    for copy in id_copies:
        copy.wait()
    live = live_ref[0, 0]
    for s in range(S):
        pos[s] = jnp.where(s < live, tin_ref[0, 0, s] * C + tout_ref[0, 0, s], -1)
    tile_copy.wait()
    cum[S] = jnp.zeros((B, B), F32)
    for s in range(S):
        prev = jnp.int32(S)
        for other_s in range(s):
            prev = jnp.where(pos[other_s] == pos[s], other_s, prev)
        term = tiles[s].astype(F32)
        cum[s] = term + cum[prev] if s else term

    def send_farther(d):
        await_token(d - 2)

        @pl.when(d < Z - 1)
        def _():
            pass_token(d - 1)

        send_feats(0, d)

    if Z > 2:
        send_farther(2)

    def place(zz, unused):
        for kk in range(2):
            for b in range(C):
                spot = (2 * zz + kk) * C + b
                last = jnp.int32(S)
                for s in range(S):
                    last = jnp.where(pos[s] == spot, s, last)
                block = cum[last]
                fwd_adj[zz, b * B:(b + 1) * B, kk * B:(kk + 1) * B] = block.astype(BF16)
                bwd_adj[2 * zz + kk, :, b * B:(b + 1) * B] = block.T.astype(BF16)
        return unused

    lax.fori_loop(0, Z, place, 0)
    each(3, Z, send_farther)
    for h in range(1, halves):
        each(2, Z, lambda d: send_feats(h, d))

    def relay(h, j):
        zz = other(j)
        feat_wait(h, 2 * zz + k)
        at_pass(zz, lambda: pass_on(h, zz).start())
        feat_forward(h, zz).start()

    def pair_feats(h, zz):
        return feat[h, pl.ds(2 * zz, 2)].reshape(2 * B, W)

    def chip_term(zz):
        for h in range(halves):
            feat_wait(h, 2 * zz + 1 - k)
        both = jnp.concatenate([pair_feats(h, zz) for h in range(halves)], axis=1)
        return dot(fwd_adj[zz], both)

    def add_chip(j):
        acc[...] += chip_term(other(j))

    def relay_all(j):
        for h in range(halves):
            relay(h, j)

    pltpu.make_async_copy(feat.at[:, r], feat.at[:, r], local_sem.at[5]).wait()
    acc[...] = chip_term(z)
    each(3, Z, lambda i: relay_all(Z + 2 - i))
    far = range(1, min(2, Z - 1) + 1)

    @pl.when(jnp.logical_and(z > 0, z < Z - 1))
    def _():
        relay_all(far[-1])

    each(3, Z, lambda i: add_chip(Z + 2 - i))

    @pl.when(jnp.logical_or(z == 0, z == Z - 1))
    def _():
        for j in far:
            relay(0, j)

    @pl.when(jnp.logical_and(z > 0, z < Z - 1))
    def _():
        for j in far[:-1]:
            relay_all(j)

    @pl.when(jnp.logical_or(z == 0, z == Z - 1))
    def _():
        for h in range(1, halves):
            for j in far:
                relay(h, j)

    for j in range(rounds):
        if j:
            for e in near:
                greet(ready.at[j], rep=c_at(e))
        pl.semaphore_wait(ready.at[j], len(near))

    def part_of(h, b):
        rows = pl.ds(pl.multiple_of(b * B, B), B)
        return acc[rows, cols(h)] + dot(fwd_adj[far_end, rows], pair_feats(h, far_end))

    def part_copy(h, e):
        return remote(
            part_send.at[h, e], part_recv.at[h, e], part_send_sem.at[0],
            part_recv_sem.at[h], rep=c_at(e),
        )

    for h in range(halves):
        if Z > 2:
            feat_wait(h, 2 * other(2) + 1 - k)
            acc[:, cols(h)] += dot(fwd_adj[other(2)], pair_feats(h, other(2)))
        feat_wait(h, 2 * far_end + 1 - k)

        def send_part(e):
            part_send[h, e] = part_of(h, c_at(e)).astype(BF16)
            part_copy(h, e).start()

        far_first(send_part)

    for h in range(halves):
        own_part[h] = part_of(h, c)

    weight_copy.wait()
    cot_copy.wait()
    weight = weight_ref[...]
    pre = None
    agg_halves = []
    for h in range(halves):

        came = part_recv.at[h, pl.ds(1, C - 1)]
        remote(came, came, part_send_sem.at[0], part_recv_sem.at[h], rep=c_at(1)).wait_recv()
        total = own_part[h]
        for e in range(1, C):
            total += part_recv[h, e].astype(F32)
        agg_half = total.astype(BF16)
        agg_halves.append(agg_half)
        term = dot(agg_half, weight[cols(h)])
        pre = term if pre is None else pre + term

    sig = jax.nn.sigmoid(pre)
    grad_pre = (cot_ref[...].astype(F32) * sig * (1.0 + pre * (1.0 - sig))).astype(BF16)

    def grad_copy(h, e):
        return remote(
            grads.at[h, c], grads.at[h, c], grad_send_sem.at[0], grad_recv_sem.at[h],
            rep=c_at(e),
        )

    def make_grads(h):
        grads[h, c] = lax.dot_general(
            grad_pre, weight[cols(h)], (((1,), (1,)), ((), ())), preferred_element_type=F32
        ).astype(BF16)

    def grad_wait(h):
        came = grads.at[h, pl.ds(0, C - 1)]
        remote(came, came, grad_send_sem.at[0], grad_recv_sem.at[h], rep=c_at(1)).wait_recv()

    def send_grads(h):
        far_first(lambda e: grad_copy(h, e).start())

    make_grads(0)
    send_grads(0)

    agg = jnp.concatenate(agg_halves, axis=1)
    w_part[...] = lax.dot_general(
        agg, grad_pre, (((0,), (0,)), ((), ())), preferred_element_type=F32
    ).reshape(w_part.shape)
    w_pair_send[...] = w_part[1 - k].astype(BF16)
    w_pair = to_partner(w_pair_send, w_pair_recv, w_pair_sem.at[0], w_pair_sem.at[1])
    w_pair.start()
    for h in range(1, halves):
        make_grads(h)
    act_ref[...] = (pre * sig).astype(BF16)

    w_pair.wait_recv()
    w_half[...] = w_part[k] + w_pair_recv[...].astype(F32)
    w_rep_send[...] = w_half[...].astype(BF16)

    def w_rep_copy(e):
        return remote(
            w_rep_send.at[c_at(e)], w_rep_recv.at[e], w_rep_sem.at[0], w_rep_sem.at[1],
            rep=c_at(e),
        )

    far_first(lambda e: w_rep_copy(e).start())
    for h in range(1, halves):
        send_grads(h)

    def ends(sent, semaphore):
        remote(sent, sent, semaphore, semaphore, row=pr).wait_send()

    skipped = [jnp.logical_and(z == 2, passing), jnp.logical_and(z == Z - 3, passing)]
    for count in range(3):
        @pl.when(sum(jnp.where(one, 1, 0) for one in skipped) == count)
        def _():
            ends(feat.at[:, pl.ds(0, Z - 1 - count)], feat_send_sem.at[0])

    for near_end in (1, Z - 2) if passing else ():
        @pl.when(z == near_end)
        def _():
            ends(feat.at[:, pl.ds(0, 1)], feat_send_sem.at[1])

    ends(feat.at[:, pl.ds(0, Z)], feat_fwd_sem.at[0])
    ends(part_send.at[:, pl.ds(1, C - 1)], part_send_sem.at[0])

    def returned(h, q):
        return dot(bwd_adj[q], grads[h].reshape(C * B, W))

    def pair_copy(h, zz):
        return to_partner(
            pair_send.at[h, zz], pair_recv.at[h, zz], pair_send_sem.at[0],
            pair_recv_sem.at[h, zz],
        )

    def ret_copy(h, zz):
        return remote(
            ret_send.at[h, zz], ret_recv.at[h, z], ret_send_sem.at[0], ret_recv_sem.at[h],
            row=2 * zz + k,
        )

    def w_z_copy(zz):
        return remote(
            w_z.at[z], w_z.at[z], w_z_sem.at[0], w_z_sem.at[1], row=2 * zz + k
        )

    def send_pair(h, zz):
        pair_send[h, zz] = returned(h, 2 * zz + 1 - k).astype(BF16)
        pair_copy(h, zz).start()

    def joined(h, zz):
        value = returned(h, 2 * zz + k)
        pair_copy(h, zz).wait_recv()
        return value + pair_recv[h, zz].astype(F32)

    def send_ret(h, j):
        zz = low_first(j)
        ret_send[h, zz] = joined(h, zz).astype(BF16)
        ret_copy(h, zz).start()

    def send_pairs(h):
        grad_wait(h)
        each(1, Z, lambda j: send_pair(h, low_first(j)))

    def own_ret(h):
        fgrad_ref[:, cols(h)] = joined(h, z)

    def send_w_z():
        came = w_rep_recv.at[pl.ds(1, C - 1)]
        remote(came, came, w_rep_sem.at[0], w_rep_sem.at[1], rep=c_at(1)).wait_recv()
        total = w_half[c]
        for e in range(1, C):
            total += w_rep_recv[e].astype(F32)
        w_z[z] = total.astype(BF16)
        each(1, Z, lambda j: w_z_copy(low_first(j)).start())

    held = (Z - 1) // 3
    send_pairs(0)
    send_w_z()
    send_pair(0, z)
    for h in range(halves):
        each(1 if h == 0 else 2, Z - held if h + 1 < halves else Z, lambda j: send_ret(h, j))
        own_ret(h)
        if h + 1 < halves:
            send_pairs(h + 1)
            send_pair(h + 1, z)
            send_ret(h + 1, 1)
            each(Z - held, Z, lambda j: send_ret(h, j))

    came = w_z.at[pl.ds(0, Z - 1)]
    remote(came, came, w_z_sem.at[0], w_z_sem.at[1], row=pr).wait_recv()
    w_all[k * C + c] = jnp.sum(w_z[...].astype(F32), axis=0).astype(BF16)

    def w_gather_copy(other_k, dst):
        mine = w_all.at[k * C + c]
        return remote(
            mine, mine, w_gather_sem.at[0], w_gather_sem.at[1],
            row=2 * z + (k + other_k) % 2, rep=dst,
        )

    def w_gather(e):
        for other_k in range(2):
            w_gather_copy(other_k, low_rep(e)).start()

    each(1, C, w_gather)
    w_gather_copy(1, c).start()

    w_pair.wait_send()
    ends(grads.at[:, pl.ds(0, C - 1)], grad_send_sem.at[0])
    ends(pair_send, pair_send_sem.at[0])
    ends(w_rep_send.at[pl.ds(0, C - 1)], w_rep_sem.at[0])
    ends(w_z.at[pl.ds(0, Z - 1)], w_z_sem.at[0])
    ends(ret_send.at[:, pl.ds(0, Z - 1)], ret_send_sem.at[0])
    most = w_all.at[pl.ds(0, 2 * C - 1)]
    ends(most, w_gather_sem.at[0])

    for h in range(halves):
        came = ret_recv.at[h, pl.ds(0, Z - 1)]
        remote(came, came, ret_send_sem.at[0], ret_recv_sem.at[h], row=pr).wait_recv()
        total = fgrad_ref[:, cols(h)]
        for j in range(1, Z):
            total += ret_recv[h, other(j)].astype(F32)
        fgrad_ref[:, cols(h)] = total
    remote(most, most, w_gather_sem.at[0], w_gather_sem.at[1], row=pr).wait_recv()
    wgrad_ref[...] = w_all[...].astype(F32).reshape(wgrad_ref.shape)


def write_out(*refs):
    count = len(refs) // 2
    sem = refs[-1]
    copies = [
        pltpu.make_async_copy(refs[i], refs[count + i], sem.at[i]) for i in range(count)
    ]
    for copy in copies:
        copy.start()
    for copy in copies:
        copy.wait()


def solution(mesh):
    R = mesh.shape["row"]
    C = mesh.shape["rep"]
    Z = R // 2

    def body(features, weight, cotangent, adjacency, tile_out, tile_in, live_count):
        B, F = features.shape
        S = adjacency.shape[2]
        H = F // (2 * C)
        N = 2
        W = F // N
        CY, CX = grid_of(C)
        anywhere = pl.BlockSpec(memory_space=pl.ANY)
        vector = pl.BlockSpec(memory_space=pltpu.VMEM)
        dma = pltpu.SemaphoreType.DMA
        out_shape = (
            jax.ShapeDtypeStruct((B, F), BF16),
            jax.ShapeDtypeStruct(weight.shape, F32),
            jax.ShapeDtypeStruct((B, F), F32),
        )
        buffers = [
            ((S, B, B), BF16), ((S + 1, B, B), F32),
            ((Z, C * B, 2 * B), BF16), ((R, B, C * B), BF16),
            ((N, R, B, W), BF16), (weight.shape, BF16), ((B, F), BF16),
            ((C * B, F), F32), ((N, B, W), F32),
            ((N, C, B, W), BF16), ((N, C, B, W), BF16), ((N, C, B, W), BF16),
            ((N, Z, B, W), BF16), ((N, Z, B, W), BF16),
            ((N, Z, B, W), BF16), ((N, Z, B, W), BF16),
            ((2, C, H, F), F32), ((C, H, F), BF16), ((C, H, F), BF16), ((C, H, F), F32),
            ((C, H, F), BF16), ((C, H, F), BF16), ((Z, H, F), BF16), ((2 * C, H, F), BF16),
        ]
        held = sum(math.prod(shape) * (4 if kind == F32 else 2) for shape, kind in buffers)
        results = pl.pallas_call(
            functools.partial(kernel, Z, C, S),
            out_shape=out_shape,
            in_specs=[pl.BlockSpec(memory_space=pltpu.HBM)] * 6
            + [pl.BlockSpec(memory_space=pltpu.SMEM)],
            out_specs=(vector, vector, vector),
            scratch_shapes=[pltpu.VMEM(shape, kind) for shape, kind in buffers] + [
                pltpu.SMEM(tile_out.shape, jnp.int32),
                pltpu.SMEM(tile_in.shape, jnp.int32),
                pltpu.SMEM((S,), jnp.int32),
                pltpu.SemaphoreType.REGULAR((max(CY // 2 + CX // 2 - 1, 1),)),
                pltpu.SemaphoreType.REGULAR((max(Z - 2, 1),)),
                dma((6,)), dma((2,)), dma((1,)), dma((N, R)),
                dma((1,)), dma((N,)), dma((1,)), dma((N,)),
                dma((1,)), dma((N, Z)), dma((1,)), dma((N,)),
                dma((2,)), dma((2,)), dma((2,)), dma((2,)),
            ],
            compiler_params=pltpu.CompilerParams(
                collective_id=0, has_side_effects=True,
                vmem_limit_bytes=min(held + 8 * 2 ** 20, 60 * 2 ** 20),
            ),
        )(*(
            pltpu.with_memory_space_constraint(arg, pltpu.HBM)
            for arg in (features, weight, cotangent, adjacency, tile_out, tile_in)
        ), live_count)
        return pl.pallas_call(
            write_out,
            out_shape=out_shape,
            in_specs=[vector] * 3,
            out_specs=(anywhere,) * 3,
            scratch_shapes=[dma((3,))],
            compiler_params=pltpu.CompilerParams(vmem_limit_bytes=4 * 2 ** 20),
        )(*results)

    return jax.shard_map(
        body,
        mesh=mesh,
        in_specs=(
            P(("row", "rep"), None),
            P(),
            P(("row", "rep"), None),
            P("row", "rep", None, None, None),
            P("row", "rep", None),
            P("row", "rep", None),
            P("row", "rep"),
        ),
        out_specs=(P(("row", "rep"), None), P(), P(("row", "rep"), None)),
        check_vma=False,
    )
```
